32 devices in a mesh: space: 16 (over z, y, core), slab: 2 (over x).
Axes of the slice: x: 2, y: 2, z: 4, core: 2. Of those that a mesh axis runs over, the one named last changes fastest.
Arguments:
- wavefunctions: bfloat16 [64, 83232], P(None, ('space', 'slab')), may hold values from -6 to 6
- kinetic: bfloat16 [729, 729], replicated, may hold values from -1 to 2, as said below
- cell_scale: float32 [128], P(('space', 'slab')), may hold values from 0.5 to 2
- potential: float32 [128, 729], P(('space', 'slab')), may hold values from -1 to 1
- cell_nodes: int32 [128, 729], P(('space', 'slab')), may hold values from 0 to 2600, as said below
- face_space: int32 [64, 289], P(('space', 'slab')), may hold values from 0 to 2600, as said below
- face_slab: int32 [64, 153], P(('space', 'slab')), may hold values from 0 to 2600, as said below
- projectors: bfloat16 [128, 18, 729], P(('space', 'slab')), may hold values from -0.21875 to 0.21875
- cell_atom: int32 [128], P(('space', 'slab')), may hold values from 0 to 7
- coupling: float32 [128, 18, 18], P(('space', 'slab')), may hold values from -8 to 8
Outputs:
- filtered: float32 [64, 83232], P(None, ('space', 'slab'))
The draws below stay inside these ranges and needn't reach their ends.
Inputs may be any that keep to these rules, and one draw needn't show every extreme that they name: `cell_nodes`: each block's 4 cells tile a block of 1 x 2 x 2 cells of degree 8; within a block the cell nodes name the nodes of that block's node grid, numbered in an order of the block's own. `face_space`: row 2b lists the nodes of block b's lower face across the long direction and row 2b + 1 those of its upper face, both in one fixed order of the face's positions, so that a block's upper face and the next block's lower face list the same nodes at equal positions; each row names distinct nodes. `face_slab`: likewise for the faces across the cross-section between blocks l and l + 1 of a row. `kinetic`: A symmetric matrix.
All inputs are finite; a program needn't handle non-finite values.
Results may differ from the reference program's by a relative error of at most 0.0039.
Values may be sent and summed in bfloat16 or wider, within the bound.
A program may use at most 64 MiB of HBM per device.

```python
import math
import jax
import jax.numpy as jnp
from jax import lax

P_SIZE = 8
NW = 64
NP = 18
CX = 1
CY = 2
CZ = 2
ASLOT = 4
ITERS = 2
NPC = 729
CELLS = 4
NODE_DEV = 2601
FS = 289
FL = 153
NODES = 83232
CELLS_ALL = 128
ATOMS = 128
N_SPACE = 16
N_SLAB = 2


def node_numbering(key):
    devices_all = N_SPACE * N_SLAB
    base = jax.random.fold_in(key, 7)
    keys = jax.vmap(lambda index: jax.random.fold_in(base, index))(jnp.arange(devices_all))
    return jax.vmap(lambda sub: jax.random.permutation(sub, NODE_DEV))(keys).astype(jnp.int32)


def canonical(grid_x, grid_y, grid_z):
    return (grid_x * (P_SIZE * CY + 1) + grid_y) * (P_SIZE * CZ + 1) + grid_z


def draw_cell_nodes(key, part):
    numbering = node_numbering(key)
    cell_index = jnp.arange(CELLS, dtype=jnp.int32)
    cell_x = cell_index // (CY * CZ)
    cell_y = cell_index // CZ % CY
    cell_z = cell_index % CZ
    local_index = jnp.arange(NPC, dtype=jnp.int32)
    node_x = local_index // ((P_SIZE + 1) * (P_SIZE + 1))
    node_y = local_index // (P_SIZE + 1) % (P_SIZE + 1)
    node_z = local_index % (P_SIZE + 1)
    canon = canonical(cell_x[:, None] * P_SIZE + node_x[None, :], cell_y[:, None] * P_SIZE + node_y[None, :], cell_z[:, None] * P_SIZE + node_z[None, :])
    result = jnp.take(numbering, canon.reshape(-1), axis=1)
    return result.reshape(N_SPACE * N_SLAB * CELLS, NPC).astype(jnp.int32)


def draw_face_space(key, part):
    numbering = node_numbering(key)
    face_index = jnp.arange(FS, dtype=jnp.int32)
    grid_y = face_index // (P_SIZE * CZ + 1)
    grid_z = face_index % (P_SIZE * CZ + 1)
    lower = canonical(jnp.zeros_like(grid_y), grid_y, grid_z)
    upper = canonical(jnp.zeros_like(grid_y) + P_SIZE * CX, grid_y, grid_z)
    both = jnp.stack([jnp.take(numbering, lower, axis=1), jnp.take(numbering, upper, axis=1)], axis=1)
    return both.reshape(2 * N_SPACE * N_SLAB, FS).astype(jnp.int32)


def draw_face_slab(key, part):
    numbering = node_numbering(key)
    face_index = jnp.arange(FL, dtype=jnp.int32)
    grid_x = face_index // (P_SIZE * CZ + 1)
    grid_z = face_index % (P_SIZE * CZ + 1)
    lower = canonical(grid_x, jnp.zeros_like(grid_x), grid_z)
    upper = canonical(grid_x, jnp.zeros_like(grid_x) + P_SIZE * CY, grid_z)
    both = jnp.stack([jnp.take(numbering, lower, axis=1), jnp.take(numbering, upper, axis=1)], axis=1)
    return both.reshape(2 * N_SPACE * N_SLAB, FL).astype(jnp.int32)


def draw_kinetic(key, part):
    base = jax.random.fold_in(key, 11)
    noise = jax.random.normal(jax.random.fold_in(base, 1), (NPC, NPC), jnp.float32)
    diagonal = jax.random.uniform(jax.random.fold_in(base, 2), (NPC,), jnp.float32, 0.5, 1.5)
    symmetric = 0.5 * (noise + noise.T) / jnp.sqrt(2.0 * NPC)
    symmetric = jnp.clip(symmetric, -0.9, 0.9)
    return (symmetric + jnp.diag(diagonal)).astype(jnp.bfloat16)


def touch_ends(array, own_key, smallest, largest):
    longest = array.shape.index(max(array.shape))
    spots = []
    for shift in (0, 1):
        where = [jax.random.randint(jax.random.fold_in(own_key, axis), (), 0, length) for axis, length in enumerate(array.shape)]
        where[longest] = (where[longest] + shift) % array.shape[longest]
        spots.append(tuple(where))
    return array.at[spots[0]].set(smallest).at[spots[1]].set(largest)


def block_scale(stream_key, extent, cuts, smallest, high):
    def one(axis_at, blocks):
        draws = jax.random.uniform(jax.random.fold_in(jax.random.fold_in(stream_key, 6), axis_at), (blocks,), jnp.float32, smallest / len(cuts), high / len(cuts))
        return jnp.repeat(jnp.exp(draws), extent[axis_at] // blocks).reshape((-1,) + (1,) * (len(extent) - axis_at - 1))

    factor_of = one(*cuts[0])
    for cut in cuts[1:]:
        factor_of = factor_of * one(*cut)
    return factor_of


def bell_draw(key, shape, scale, most, split=(), held_as=jnp.bfloat16):
    entries = jax.random.normal(key, shape, jnp.float32) * scale
    if len(split) > 0:
        entries = block_scale(key, shape, split, -0.22, 0.18) * entries
    return jnp.clip(entries, min=-most, max=most).astype(held_as)


def setup_inputs(seed: int = 0) -> dict:
    arg_keys = jax.random.split(jax.random.key(seed), 11)
    wavefunctions = bell_draw(arg_keys[0], (NW, NODES), 1.0, 6.0, ((1, 32),))
    kinetic = draw_kinetic(jax.random.fold_in(arg_keys[10], 71), 0)
    cell_scale = jnp.clip(jnp.exp(math.log(2.0) - 1.3862944 * jax.random.uniform(arg_keys[2], (CELLS_ALL,), jnp.float32) ** block_scale(arg_keys[2], (CELLS_ALL,), ((0, 32),), -0.2, 0.2)), 0.5, 2.0)
    potential = jnp.clip(jax.random.uniform(arg_keys[3], (CELLS_ALL, NPC), jnp.float32, -1.0, 1.0) * block_scale(arg_keys[3], (CELLS_ALL, NPC), ((0, 32),), -0.4, 0.0), -1.0, 1.0)
    cell_nodes = draw_cell_nodes(jax.random.fold_in(arg_keys[10], 71), 0)
    face_space = draw_face_space(jax.random.fold_in(arg_keys[10], 71), 0)
    face_slab = draw_face_slab(jax.random.fold_in(arg_keys[10], 71), 0)
    projectors = bell_draw(arg_keys[7], (CELLS_ALL, NP, NPC), NPC ** -0.5, 0.21875, ((0, 32),))
    cell_atom = touch_ends(jax.random.randint(arg_keys[8], (CELLS_ALL,), 0, N_SLAB * ASLOT), jax.random.fold_in(arg_keys[8], 1), 0, (N_SLAB * ASLOT) - 1).astype(jnp.int32)
    coupling = bell_draw(arg_keys[9], (ATOMS, NP, NP), 2.0, 8.0, ((0, 32),), jnp.float32)
    return dict(wavefunctions=wavefunctions, kinetic=kinetic, cell_scale=cell_scale, potential=potential, cell_nodes=cell_nodes, face_space=face_space, face_slab=face_slab, projectors=projectors, cell_atom=cell_atom, coupling=coupling)


filter_centre = 8.0
filter_half = 8.0


def cell_values_of(field_dev, nodes_dev):
    values = jnp.take(field_dev, nodes_dev.reshape(-1), axis=1).astype(jnp.bfloat16)
    return values.reshape(NW, CELLS, NPC)


def margins_dev(inputs):
    field_dev, nodes_dev, projector_dev, atom_dev = inputs
    values = cell_values_of(field_dev, nodes_dev).astype(jnp.float32)
    margin = jnp.einsum("wcj,cpj->cpw", values, projector_dev.astype(jnp.float32))
    onehot = (atom_dev[:, None] == jnp.arange(N_SLAB * ASLOT, dtype=jnp.int32)[None, :]).astype(jnp.float32)
    return jnp.einsum("ca,cpw->apw", onehot, margin, precision=lax.Precision.HIGHEST)


def apply_dev(inputs, kinetic):
    field_dev, nodes_dev, projector_dev, atom_dev, scale_dev, potential_dev, coupled_row = inputs
    values = cell_values_of(field_dev, nodes_dev).astype(jnp.float32)
    kinetic_part = jnp.einsum("wcj,jk->wck", values, kinetic.astype(jnp.float32))
    per_cell = coupled_row[atom_dev].astype(jnp.float32)
    nonlocal_part = jnp.einsum("cpw,cpj->wcj", per_cell, projector_dev.astype(jnp.float32))
    total = scale_dev[None, :, None] * kinetic_part + potential_dev[None] * values + nonlocal_part
    zeros_field = jnp.zeros((NW, NODE_DEV), jnp.float32)
    return zeros_field.at[:, nodes_dev.reshape(-1)].add(total.reshape(NW, CELLS * NPC))


def take_faces(grid, index_grid):
    shape_full = grid.shape[:3] + (index_grid.shape[-1],)
    return jnp.take_along_axis(grid, jnp.broadcast_to(index_grid[:, :, None, :], shape_full), axis=3)


def add_faces(grid, lower_idx, upper_idx, add_lower, add_upper):
    def add_one(inputs):
        field_dev, idx_low, idx_high, value_low, value_high = inputs
        return field_dev.at[:, idx_low].add(value_low).at[:, idx_high].add(value_high)

    flat = lambda arr: arr.reshape((N_SPACE * N_SLAB,) + arr.shape[2:])
    result = lax.map(add_one, (flat(grid), flat(lower_idx), flat(upper_idx), flat(add_lower), flat(add_upper)))
    return result.reshape(grid.shape)


def space_sum(grid, faces):
    lower_vals = take_faces(grid, faces[:, :, 0])
    upper_vals = take_faces(grid, faces[:, :, 1])
    zeros_row = jnp.zeros_like(lower_vals[:1])
    from_below = jnp.concatenate([zeros_row, upper_vals[:-1]], axis=0)
    from_above = jnp.concatenate([lower_vals[1:], zeros_row], axis=0)
    return add_faces(grid, faces[:, :, 0], faces[:, :, 1], from_below, from_above)


def slab_sum(grid, faces):
    lower_vals = take_faces(grid, faces[:, :, 0])
    upper_vals = take_faces(grid, faces[:, :, 1])
    zeros_col = jnp.zeros_like(lower_vals[:, :1])
    from_below = jnp.concatenate([zeros_col, upper_vals[:, :-1]], axis=1)
    from_above = jnp.concatenate([lower_vals[:, 1:], zeros_col], axis=1)
    return add_faces(grid, faces[:, :, 0], faces[:, :, 1], from_below, from_above)


def reference(wavefunctions, kinetic, cell_scale, potential, cell_nodes, face_space, face_slab, projectors, cell_atom, coupling):
    devices_all = N_SPACE * N_SLAB
    nodes_r = cell_nodes.reshape(devices_all, CELLS, NPC)
    projector_r = projectors.reshape(devices_all, CELLS, NP, NPC)
    atom_r = cell_atom.reshape(devices_all, CELLS)
    scale_r = cell_scale.reshape(devices_all, CELLS)
    potential_r = potential.reshape(devices_all, CELLS, NPC)
    space_faces = face_space.reshape(N_SPACE, N_SLAB, 2, FS)
    slab_faces = face_slab.reshape(N_SPACE, N_SLAB, 2, FL)
    coupling_r = coupling.reshape(N_SPACE, N_SLAB * ASLOT, NP, NP)

    def operate(fields):
        partials = lax.map(margins_dev, (fields, nodes_r, projector_r, atom_r))
        rows = partials.reshape(N_SPACE, N_SLAB, N_SLAB * ASLOT, NP, NW).sum(axis=1)
        coupled = jnp.einsum("raqp,rapw->raqw", coupling_r, rows, precision=lax.Precision.HIGHEST).astype(jnp.bfloat16)
        coupled_dev = jnp.repeat(coupled, N_SLAB, axis=0)
        assembled = lax.map(lambda inputs: apply_dev(inputs, kinetic), (fields, nodes_r, projector_r, atom_r, scale_r, potential_r, coupled_dev))
        grid = assembled.reshape(N_SPACE, N_SLAB, NW, NODE_DEV)
        grid = space_sum(grid, space_faces)
        grid = slab_sum(grid, slab_faces)
        return grid.reshape(devices_all, NW, NODE_DEV)

    start = wavefunctions.astype(jnp.float32).reshape(NW, devices_all, NODE_DEV).transpose(1, 0, 2)
    previous = start
    current = (operate(start) - filter_centre * start) / filter_half
    for step_index in range(ITERS - 1):
        following = 2.0 * (operate(current) - filter_centre * current) / filter_half - previous
        previous = current
        current = following
    return current.transpose(1, 0, 2).reshape(NW, NODES)
```

```python
import functools

import jax
import jax.numpy as jnp
from jax import lax
from jax.experimental import pallas as pl
from jax.experimental.pallas import tpu as pltpu
from jax.sharding import PartitionSpec as P

filter_centre = 8.0
filter_half = 8.0
BLK = 256
MESH = pl.DeviceIdType.MESH
NT = (((1,), (1,)), ((), ()))
f32 = jnp.float32
bf16 = jnp.bfloat16


def up(value, unit):
    return -(-value // unit) * unit


def kernel(
    dims,
    y_ref,
    kin_ref,
    scale_ref,
    pot_ref,
    cn_ref,
    fs_ref,
    fl_ref,
    pr_ref,
    pack_ref,
    out_ref,
    hot,
    idx,
    kin,
    pp,
    pot,
    cross,
    packs,
    coup,
    yb,
    vals,
    tot,
    asm,
    asmb,
    asm2,
    outg,
    in_space,
    in_slab,
    inc,
    marg,
    pack_send,
    pack_recv,
    marg_send,
    marg_recv,
    face_send,
    face_recv,
):
    n_space, n_slab = dims["n_space"], dims["n_slab"]
    width, nodes, cells, order = dims["width"], dims["nodes"], dims["cells"], dims["order"]
    atoms, nproj, pstride = dims["atoms"], dims["nproj"], dims["pstride"]
    fs, fl = dims["fs"], dims["fl"]
    op, npad = up(order, BLK), up(nodes, BLK)
    fsp, flp = up(fs, 128), up(fl, 128)
    jp = cells * op
    fp = up(2 * fsp + 2 * flp, BLK)
    lp = cells * pstride
    o_sl = 2 * fsp

    s = lax.axis_index("space")
    l = lax.axis_index("slab")
    above, below = lax.rem(s + 1, n_space), lax.rem(s + n_space - 1, n_space)
    right, left = lax.rem(l + 1, n_slab), lax.rem(l + n_slab - 1, n_slab)

    barrier = pltpu.get_barrier_semaphore()
    for d in range(1, n_slab):
        pl.semaphore_signal(
            barrier, inc=1, device_id={"slab": lax.rem(l + d, n_slab)}, device_id_type=MESH
        )
    for t in (above, below):
        pl.semaphore_signal(barrier, inc=1, device_id={"space": t}, device_id_type=MESH)
    pl.semaphore_wait(barrier, n_slab + 1)

    pack_copies = []
    for d in range(1, n_slab):
        copy = pltpu.make_async_remote_copy(
            src_ref=pack_ref,
            dst_ref=packs.at[d - 1],
            send_sem=pack_send.at[d - 1],
            recv_sem=pack_recv.at[d - 1],
            device_id={"slab": lax.rem(l + d, n_slab)},
            device_id_type=MESH,
        )
        copy.start()
        pack_copies.append(copy)

    idx[...] = jnp.full(idx.shape, -1, jnp.int32)
    for c in range(cells):
        idx[0:1, c * op : c * op + order] = cn_ref[c : c + 1, :]
    for k in range(2):
        idx[0:1, jp + k * fsp : jp + k * fsp + fs] = fs_ref[k : k + 1, :]
        off = jp + o_sl + k * flp
        idx[0:1, off : off + fl] = fl_ref[k : k + 1, :]

    kin[...] = jnp.zeros(kin.shape, bf16)
    kin[0:order, 0:order] = kin_ref[...]
    pp[...] = jnp.zeros(pp.shape, bf16)
    pot[...] = jnp.zeros(pot.shape, f32)
    pot[0:cells, 0:order] = pot_ref[...]
    yb[...] = jnp.zeros(yb.shape, bf16)
    yb[:, 0:nodes] = y_ref[...]
    for c in range(cells):
        pp[c * pstride : c * pstride + nproj, c * op : c * op + order] = pr_ref[c]

    @pl.loop(0, npad // BLK)
    def _(b):
        rows = lax.broadcasted_iota(jnp.int32, (BLK, BLK), 0).astype(f32).astype(bf16)
        for j in range((jp + fp) // BLK):
            cols = slice(j * BLK, (j + 1) * BLK)
            shifted = (idx[0:1, cols] - b * BLK).astype(f32).astype(bf16)
            hit = rows == jnp.broadcast_to(shifted, (BLK, BLK))
            hot[pl.ds(pl.multiple_of(b * BLK, BLK), BLK), cols] = jnp.where(
                hit, jnp.ones((), bf16), jnp.zeros((), bf16)
            )

    slab_row = idx[0:1, jp + o_sl : jp + o_sl + 2 * flp].astype(f32)
    slab_row = jnp.where(slab_row < 0, -2.0, slab_row)
    for k in range(2 * fsp // 128):
        row = idx[0:1, jp + k * 128 : jp + (k + 1) * 128].astype(f32)
        col = jnp.broadcast_to(row, (128, 128)).T
        cross[k * 128 : (k + 1) * 128, :] = jnp.where(col[:, 0:1] == slab_row, 1.0, 0.0).astype(bf16)

    for copy in pack_copies:
        copy.wait()
    own_row = pack_ref[atoms * pstride : atoms * pstride + 1, :]
    own_col = jnp.broadcast_to(own_row, (lp, lp)).T
    chosen = jnp.zeros((lp, lp), f32)
    for d in range(n_slab):
        source = lax.rem(l + n_slab - d, n_slab)
        for i in range(atoms):
            part = slice(i * pstride, (i + 1) * pstride)
            block = pack_ref[part, :] if d == 0 else packs[d - 1, part, :]
            tiled = jnp.concatenate([block] * cells, axis=0)
            chosen += jnp.where(own_col == (source * atoms + i).astype(f32), tiled, 0.0)
    for d in range(n_slab):
        last = slice(atoms * pstride, atoms * pstride + 1)
        row = pack_ref[last, :] if d == 0 else packs[d - 1, last, :]
        coup[d] = jnp.where(own_col == row, chosen, 0.0)

    lanes = lax.broadcasted_iota(jnp.int32, (1, fp), 1)
    has_below, has_above = s > 0, s < n_space - 1
    has_left, has_right = l > 0, l < n_slab - 1
    keep = (
        ((lanes < fsp) & has_below)
        | ((lanes >= fsp) & (lanes < o_sl) & has_above)
        | ((lanes >= o_sl) & (lanes < o_sl + flp) & has_left)
        | ((lanes >= o_sl + flp) & (lanes < o_sl + 2 * flp) & has_right)
    ).astype(f32)

    inc[...] = jnp.zeros(inc.shape, bf16)

    def face_copy(step, which, src, landing, device):
        count = landing.shape[-1]
        return pltpu.make_async_remote_copy(
            src_ref=outg.at[step, :, src : src + count],
            dst_ref=landing.at[step, which % 2],
            send_sem=face_send.at[step, which],
            recv_sem=face_recv.at[step, which],
            device_id=device,
            device_id_type=MESH,
        )

    for step in range(2):
        for c in range(cells):
            @pl.loop(0, op // BLK)
            def _(j, c=c):
                at = pl.ds(pl.multiple_of(c * op + j * BLK, BLK), BLK)
                got = jnp.dot(yb[...], hot[:, at], preferred_element_type=f32)
                to = pl.ds(pl.multiple_of(j * BLK, BLK), BLK)
                vals[c * width : (c + 1) * width, to] = got.astype(bf16)

        margin = jnp.zeros((width, lp), f32)
        for c in range(cells):
            margin += lax.dot_general(
                vals[c * width : (c + 1) * width, :],
                pp[:, c * op : (c + 1) * op],
                NT,
                preferred_element_type=f32,
            )
        marg[step, 0] = margin
        marg_copies = []
        for d in range(1, n_slab):
            copy = pltpu.make_async_remote_copy(
                src_ref=marg.at[step, 0],
                dst_ref=marg.at[step, d],
                send_sem=marg_send.at[step, d - 1],
                recv_sem=marg_recv.at[step, d - 1],
                device_id={"slab": lax.rem(l + d, n_slab)},
                device_id_type=MESH,
            )
            copy.start()
            marg_copies.append(copy)

        asm_kin = jnp.dot(vals[...], kin[...], preferred_element_type=f32)
        for c in range(cells):
            v = vals[c * width : (c + 1) * width, :].astype(f32)
            asm[:, c * op : (c + 1) * op] = (
                scale_ref[c] * asm_kin[c * width : (c + 1) * width] + pot[c : c + 1, :] * v
            )
        coupled = lax.dot_general(
            margin, coup[0], NT, precision=lax.Precision.HIGHEST, preferred_element_type=f32
        )
        for d in range(1, n_slab):
            marg_copies[d - 1].wait()
            coupled += lax.dot_general(
                marg[step, d], coup[d], NT, precision=lax.Precision.HIGHEST, preferred_element_type=f32
            )
        coupled = coupled.astype(bf16)
        for c in range(cells):
            cols = slice(c * op, (c + 1) * op)
            total = asm[:, cols] + jnp.dot(coupled, pp[:, cols], preferred_element_type=f32)
            high = total.astype(bf16)
            tot[0:width, cols] = high
            tot[width:, cols] = (total - high.astype(f32)).astype(bf16)

        @pl.loop(0, npad // BLK)
        def _(b):
            at = pl.ds(pl.multiple_of(b * BLK, BLK), BLK)
            both = lax.dot_general(tot[...], hot[at, 0:jp], NT, preferred_element_type=f32)
            summed = both[0:width] + both[width:]
            asm[:, at] = summed
            asmb[:, at] = summed.astype(bf16)

        @pl.loop(0, fp // BLK)
        def _(b):
            at = pl.ds(pl.multiple_of(jp + b * BLK, BLK), BLK)
            to = pl.ds(pl.multiple_of(b * BLK, BLK), BLK)
            got = jnp.dot(asmb[...], hot[:, at], preferred_element_type=f32)
            outg[step, :, to] = got.astype(bf16)

        space_copies = [
            face_copy(step, 0, fsp, in_space, {"space": above}),
            face_copy(step, 1, 0, in_space, {"space": below}),
        ]
        for copy in space_copies:
            copy.start()
        for k, copy in enumerate(space_copies):
            copy.wait()
            part = slice(k * fsp, (k + 1) * fsp)
            inc[:, part] = (in_space[step, k].astype(f32) * keep[:, part]).astype(bf16)
        extra = jnp.dot(inc[:, 0:o_sl], cross[...], preferred_element_type=f32)
        part = slice(o_sl, o_sl + 2 * flp)
        outg[step, :, part] = (outg[step, :, part].astype(f32) + extra).astype(bf16)
        slab_copies = [
            face_copy(step, 2, o_sl + flp, in_slab, {"slab": right}),
            face_copy(step, 3, o_sl, in_slab, {"slab": left}),
        ]
        for copy in slab_copies:
            copy.start()
        for k, copy in enumerate(slab_copies):
            copy.wait()
            part = slice(o_sl + k * flp, o_sl + (k + 1) * flp)
            inc[:, part] = (in_slab[step, k].astype(f32) * keep[:, part]).astype(bf16)

        if step == 0:
            @pl.loop(0, npad // BLK)
            def _(b):
                at = pl.ds(pl.multiple_of(b * BLK, BLK), BLK)
                added = lax.dot_general(
                    inc[...], hot[at, jp : jp + fp], NT, preferred_element_type=f32
                )
                start = yb[:, at].astype(f32)
                current = (asm[:, at] + added - filter_centre * start) / filter_half
                asm2[:, at] = -2.0 * filter_centre * current / filter_half - start
                yb[:, at] = current.astype(bf16)
        else:
            def final(at):
                added = lax.dot_general(
                    inc[...], hot[at, jp : jp + fp], NT, preferred_element_type=f32
                )
                return 2.0 * (asm[:, at] + added) / filter_half + asm2[:, at]

            @pl.loop(0, nodes // BLK)
            def _(b):
                at = pl.ds(pl.multiple_of(b * BLK, BLK), BLK)
                out_ref[:, at] = final(at)

            if nodes % BLK:
                low = nodes // BLK * BLK
                out_ref[:, low:nodes] = final(slice(low, low + BLK))[:, 0 : nodes - low]


def shards(
    wavefunctions,
    kinetic,
    cell_scale,
    potential,
    cell_nodes,
    face_space,
    face_slab,
    projectors,
    cell_atom,
    coupling,
):
    width, nodes = wavefunctions.shape
    cells, order = cell_nodes.shape
    atoms, nproj = coupling.shape[0], coupling.shape[1]
    n_space, n_slab = lax.axis_size("space"), lax.axis_size("slab")
    fs, fl = face_space.shape[1], face_slab.shape[1]
    pstride = up(nproj, 16)
    while cells * pstride % 128:
        pstride += 16
    dims = dict(
        n_space=n_space, n_slab=n_slab, width=width, nodes=nodes, cells=cells, order=order,
        atoms=atoms, nproj=nproj, pstride=pstride, fs=fs, fl=fl,
    )
    op, npad = up(order, BLK), up(nodes, BLK)
    fsp, flp = up(fs, 128), up(fl, 128)
    jp = cells * op
    fp = up(2 * fsp + 2 * flp, BLK)
    lp = cells * pstride
    extra = pstride - nproj
    padded = jnp.pad(coupling, ((0, 0), (0, extra), (0, extra)))
    tiled = jnp.tile(padded, (1, 1, cells)).reshape(atoms * pstride, lp)
    atom_row = jnp.repeat(cell_atom.astype(f32), pstride)
    pack = jnp.concatenate([tiled, jnp.broadcast_to(atom_row[None], (8, lp))], axis=0)
    others = max(n_slab - 1, 1)
    vmem = pl.BlockSpec(memory_space=pltpu.VMEM)
    smem = pl.BlockSpec(memory_space=pltpu.SMEM)
    dma = pltpu.SemaphoreType.DMA
    return pl.pallas_call(
        functools.partial(kernel, dims),
        out_shape=jax.ShapeDtypeStruct((width, nodes), f32),
        in_specs=[vmem, vmem, smem] + [vmem] * 6,
        out_specs=vmem,
        scratch_shapes=[
            pltpu.VMEM((npad, jp + fp), bf16),
            pltpu.VMEM((8, jp + fp), jnp.int32),
            pltpu.VMEM((op, op), bf16),
            pltpu.VMEM((lp, jp), bf16),
            pltpu.VMEM((up(cells, 8), op), f32),
            pltpu.VMEM((2 * fsp, 2 * flp), bf16),
            pltpu.VMEM((others, atoms * pstride + 8, lp), f32),
            pltpu.VMEM((n_slab, lp, lp), f32),
            pltpu.VMEM((width, npad), bf16),
            pltpu.VMEM((cells * width, op), bf16),
            pltpu.VMEM((2 * width, jp), bf16),
            pltpu.VMEM((width, max(jp, npad)), f32),
            pltpu.VMEM((width, npad), bf16),
            pltpu.VMEM((width, npad), f32),
            pltpu.VMEM((2, width, fp), bf16),
            pltpu.VMEM((2, 2, width, fsp), bf16),
            pltpu.VMEM((2, 2, width, flp), bf16),
            pltpu.VMEM((width, fp), bf16),
            pltpu.VMEM((2, n_slab, width, lp), f32),
            dma((others,)),
            dma((others,)),
            dma((2, others)),
            dma((2, others)),
            dma((2, 4)),
            dma((2, 4)),
        ],
        compiler_params=pltpu.CompilerParams(
            collective_id=0, has_side_effects=True, vmem_limit_bytes=60 * 1024 * 1024
        ),
    )(
        wavefunctions, kinetic, cell_scale, potential, cell_nodes, face_space, face_slab,
        projectors, pack,
    )


def solution(mesh):
    placed = (
        P(None, ("space", "slab")),
        P(),
        P(("space", "slab")),
        P(("space", "slab"), None),
        P(("space", "slab"), None),
        P(("space", "slab"), None),
        P(("space", "slab"), None),
        P(("space", "slab"), None, None),
        P(("space", "slab")),
        P(("space", "slab"), None, None),
    )
    return jax.shard_map(
        shards, mesh=mesh, in_specs=placed, out_specs=P(None, ("space", "slab")), check_vma=False
    )
```

```python
import functools

import jax
import jax.numpy as jnp
from jax import lax
from jax.experimental import pallas as pl
from jax.experimental.pallas import tpu as pltpu
from jax.sharding import PartitionSpec as P

filter_centre = 8.0
filter_half = 8.0
BLK = 256
MESH = pl.DeviceIdType.MESH
NT = (((1,), (1,)), ((), ()))
f32 = jnp.float32
bf16 = jnp.bfloat16


def up(value, unit):
    return -(-value // unit) * unit


def kernel(
    dims,
    y_ref,
    kin_ref,
    scale_ref,
    pot_ref,
    cn_ref,
    fs_ref,
    fl_ref,
    pr_ref,
    atom_ref,
    coupling_ref,
    out_ref,
    hot,
    hotf,
    pack,
    idx,
    kin,
    pp,
    pot,
    cross,
    packs,
    coup,
    yb,
    vals,
    tot,
    asm,
    asmb,
    asm2,
    outg,
    in_space,
    in_slab,
    inc,
    marg,
    pack_send,
    pack_recv,
    marg_send,
    marg_recv,
    face_send,
    face_recv,
):
    n_space, n_slab = dims["n_space"], dims["n_slab"]
    width, nodes, cells, order = dims["width"], dims["nodes"], dims["cells"], dims["order"]
    atoms, nproj, pstride = dims["atoms"], dims["nproj"], dims["pstride"]
    fs, fl = dims["fs"], dims["fl"]
    op, npad = up(order, BLK), up(nodes, BLK)
    fsp, flp = up(fs, 128), up(fl, 128)
    jp = cells * op
    fp = up(2 * fsp + 2 * flp, BLK)
    lp = cells * pstride
    o_sl = 2 * fsp

    s = lax.axis_index("space")
    l = lax.axis_index("slab")
    above, below = lax.rem(s + 1, n_space), lax.rem(s + n_space - 1, n_space)
    right, left = lax.rem(l + 1, n_slab), lax.rem(l + n_slab - 1, n_slab)

    lane_cell = lax.broadcasted_iota(jnp.int32, (8, lp), 1) // pstride
    atom_row = jnp.zeros((8, lp), f32)
    for c in range(cells):
        atom_row = jnp.where(lane_cell == c, atom_ref[c].astype(f32), atom_row)
    pack[...] = jnp.zeros(pack.shape, f32)
    for i in range(atoms):
        part = slice(i * pstride, (i + 1) * pstride)
        pack[i * pstride : i * pstride + nproj, 0:nproj] = coupling_ref[:, i, :]
        once = pack[part, :]
        many = once
        for c in range(1, cells):
            many = many + pltpu.roll(once, c * pstride, 1)
        pack[part, :] = many
    pack[atoms * pstride :, :] = atom_row

    barrier = pltpu.get_barrier_semaphore()
    for d in range(1, n_slab):
        pl.semaphore_signal(
            barrier, inc=1, device_id={"slab": lax.rem(l + d, n_slab)}, device_id_type=MESH
        )
    for t in (above, below):
        pl.semaphore_signal(barrier, inc=1, device_id={"space": t}, device_id_type=MESH)
    pl.semaphore_wait(barrier, n_slab + 1)

    pack_copies = []
    for d in range(1, n_slab):
        copy = pltpu.make_async_remote_copy(
            src_ref=pack,
            dst_ref=packs.at[d - 1],
            send_sem=pack_send.at[d - 1],
            recv_sem=pack_recv.at[d - 1],
            device_id={"slab": lax.rem(l + d, n_slab)},
            device_id_type=MESH,
        )
        copy.start()
        pack_copies.append(copy)

    idx[...] = jnp.full(idx.shape, -1, jnp.int32)
    for c in range(cells):
        idx[0:1, c * op : c * op + order] = cn_ref[c : c + 1, :]
    for k in range(2):
        idx[0:1, jp + k * fsp : jp + k * fsp + fs] = fs_ref[k : k + 1, :]
        off = jp + o_sl + k * flp
        idx[0:1, off : off + fl] = fl_ref[k : k + 1, :]

    kin[...] = jnp.zeros(kin.shape, bf16)
    kin[0:order, 0:order] = kin_ref[...]
    pp[...] = jnp.zeros(pp.shape, bf16)
    pot[...] = jnp.zeros(pot.shape, f32)
    pot[0:cells, 0:order] = pot_ref[...]
    yb[...] = jnp.zeros(yb.shape, bf16)
    yb[:, 0:nodes] = y_ref[...]
    for c in range(cells):
        pp[c * pstride : c * pstride + nproj, c * op : c * op + order] = pr_ref[:, c, :]

    rows = lax.broadcasted_iota(jnp.int32, (BLK, BLK), 0).astype(f32).astype(bf16)

    def one_hot(index_row, b):
        shifted = (index_row - b * BLK).astype(f32).astype(bf16)
        hit = rows == jnp.broadcast_to(shifted, (BLK, BLK))
        return jnp.where(hit, jnp.ones((), bf16), jnp.zeros((), bf16))

    per_cell = op // BLK

    @pl.loop(0, cells * per_cell)
    def _(j):
        at = pl.ds(pl.multiple_of(j * BLK, BLK), BLK)
        index_row = idx[0:1, at]
        got = jnp.zeros((width, BLK), f32)
        for b in range(npad // BLK):
            part = slice(b * BLK, (b + 1) * BLK)
            block = one_hot(index_row, b)
            hot[part, at] = block
            got += jnp.dot(yb[:, part], block, preferred_element_type=f32)
        row = pl.ds(pl.multiple_of(j // per_cell * width, width), width)
        to = pl.ds(pl.multiple_of(j % per_cell * BLK, BLK), BLK)
        vals[row, to] = got.astype(bf16)

    slab_row = idx[0:1, jp + o_sl : jp + o_sl + 2 * flp].astype(f32)
    slab_row = jnp.where(slab_row < 0, -2.0, slab_row)
    for k in range(2 * fsp // 128):
        row = idx[0:1, jp + k * 128 : jp + (k + 1) * 128].astype(f32)
        col = jnp.broadcast_to(row, (128, 128)).T
        cross[k * 128 : (k + 1) * 128, :] = jnp.where(col[:, 0:1] == slab_row, 1.0, 0.0).astype(bf16)

    for copy in pack_copies:
        copy.wait()
    own_row = pack[atoms * pstride : atoms * pstride + 1, :]
    own_col = jnp.broadcast_to(own_row, (lp, lp)).T
    chosen = jnp.zeros((lp, lp), f32)
    for d in range(n_slab):
        source = lax.rem(l + n_slab - d, n_slab)
        for i in range(atoms):
            part = slice(i * pstride, (i + 1) * pstride)
            block = pack[part, :] if d == 0 else packs[d - 1, part, :]
            tiled = jnp.concatenate([block] * cells, axis=0)
            chosen += jnp.where(own_col == (source * atoms + i).astype(f32), tiled, 0.0)
    for d in range(n_slab):
        last = slice(atoms * pstride, atoms * pstride + 1)
        row = pack[last, :] if d == 0 else packs[d - 1, last, :]
        coup[d] = jnp.where(own_col == row, chosen, 0.0)

    lanes = lax.broadcasted_iota(jnp.int32, (1, fp), 1)
    has_below, has_above = s > 0, s < n_space - 1
    has_left, has_right = l > 0, l < n_slab - 1
    keep = (
        ((lanes < fsp) & has_below)
        | ((lanes >= fsp) & (lanes < o_sl) & has_above)
        | ((lanes >= o_sl) & (lanes < o_sl + flp) & has_left)
        | ((lanes >= o_sl + flp) & (lanes < o_sl + 2 * flp) & has_right)
    ).astype(f32)

    inc[...] = jnp.zeros(inc.shape, bf16)

    def face_copy(step, which, src, landing, device):
        count = landing.shape[-1]
        return pltpu.make_async_remote_copy(
            src_ref=outg.at[step, :, src : src + count],
            dst_ref=landing.at[step, which % 2],
            send_sem=face_send.at[step, which],
            recv_sem=face_recv.at[step, which],
            device_id=device,
            device_id_type=MESH,
        )

    for step in range(2):
        if step > 0:
            @pl.loop(0, cells * per_cell)
            def _(j):
                at = pl.ds(pl.multiple_of(j * BLK, BLK), BLK)
                got = jnp.dot(yb[...], hot[:, at], preferred_element_type=f32)
                row = pl.ds(pl.multiple_of(j // per_cell * width, width), width)
                to = pl.ds(pl.multiple_of(j % per_cell * BLK, BLK), BLK)
                vals[row, to] = got.astype(bf16)

        margin = jnp.zeros((width, lp), f32)
        for c in range(cells):
            margin += lax.dot_general(
                vals[c * width : (c + 1) * width, :],
                pp[:, c * op : (c + 1) * op],
                NT,
                preferred_element_type=f32,
            )
        marg[step, 0] = margin
        marg_copies = []
        for d in range(1, n_slab):
            copy = pltpu.make_async_remote_copy(
                src_ref=marg.at[step, 0],
                dst_ref=marg.at[step, d],
                send_sem=marg_send.at[step, d - 1],
                recv_sem=marg_recv.at[step, d - 1],
                device_id={"slab": lax.rem(l + d, n_slab)},
                device_id_type=MESH,
            )
            copy.start()
            marg_copies.append(copy)

        asm_kin = jnp.dot(vals[...], kin[...], preferred_element_type=f32)
        for c in range(cells):
            v = vals[c * width : (c + 1) * width, :].astype(f32)
            asm[:, c * op : (c + 1) * op] = (
                scale_ref[c] * asm_kin[c * width : (c + 1) * width] + pot[c : c + 1, :] * v
            )
        coupled = lax.dot_general(
            margin, coup[0], NT, precision=lax.Precision.HIGHEST, preferred_element_type=f32
        )
        for d in range(1, n_slab):
            marg_copies[d - 1].wait()
            coupled += lax.dot_general(
                marg[step, d], coup[d], NT, precision=lax.Precision.HIGHEST, preferred_element_type=f32
            )
        coupled = coupled.astype(bf16)
        for c in range(cells):
            cols = slice(c * op, (c + 1) * op)
            total = asm[:, cols] + jnp.dot(coupled, pp[:, cols], preferred_element_type=f32)
            high = total.astype(bf16)
            tot[0:width, cols] = high
            tot[width:, cols] = (total - high.astype(f32)).astype(bf16)

        @pl.loop(0, npad // BLK)
        def _(b):
            at = pl.ds(pl.multiple_of(b * BLK, BLK), BLK)
            if step == 0:
                for j in range(fp // BLK):
                    hotf[at, j * BLK : (j + 1) * BLK] = one_hot(
                        idx[0:1, jp + j * BLK : jp + (j + 1) * BLK], b
                    )
            both = lax.dot_general(tot[...], hot[at, :], NT, preferred_element_type=f32)
            summed = both[0:width] + both[width:]
            asm[:, at] = summed
            asmb[:, at] = summed.astype(bf16)

        @pl.loop(0, fp // BLK)
        def _(b):
            to = pl.ds(pl.multiple_of(b * BLK, BLK), BLK)
            got = jnp.dot(asmb[...], hotf[:, to], preferred_element_type=f32)
            outg[step, :, to] = got.astype(bf16)

        space_copies = [
            face_copy(step, 0, fsp, in_space, {"space": above}),
            face_copy(step, 1, 0, in_space, {"space": below}),
        ]
        for copy in space_copies:
            copy.start()
        for k, copy in enumerate(space_copies):
            copy.wait()
            part = slice(k * fsp, (k + 1) * fsp)
            inc[:, part] = (in_space[step, k].astype(f32) * keep[:, part]).astype(bf16)
        extra = jnp.dot(inc[:, 0:o_sl], cross[...], preferred_element_type=f32)
        part = slice(o_sl, o_sl + 2 * flp)
        outg[step, :, part] = (outg[step, :, part].astype(f32) + extra).astype(bf16)
        slab_copies = [
            face_copy(step, 2, o_sl + flp, in_slab, {"slab": right}),
            face_copy(step, 3, o_sl, in_slab, {"slab": left}),
        ]
        for copy in slab_copies:
            copy.start()
        for k, copy in enumerate(slab_copies):
            copy.wait()
            part = slice(o_sl + k * flp, o_sl + (k + 1) * flp)
            inc[:, part] = (in_slab[step, k].astype(f32) * keep[:, part]).astype(bf16)

        if step == 0:
            @pl.loop(0, npad // BLK)
            def _(b):
                at = pl.ds(pl.multiple_of(b * BLK, BLK), BLK)
                added = lax.dot_general(
                    inc[...], hotf[at, :], NT, preferred_element_type=f32
                )
                start = yb[:, at].astype(f32)
                current = (asm[:, at] + added - filter_centre * start) / filter_half
                asm2[:, at] = -2.0 * filter_centre * current / filter_half - start
                yb[:, at] = current.astype(bf16)
        else:
            def final(at):
                added = lax.dot_general(
                    inc[...], hotf[at, :], NT, preferred_element_type=f32
                )
                return 2.0 * (asm[:, at] + added) / filter_half + asm2[:, at]

            @pl.loop(0, nodes // BLK)
            def _(b):
                at = pl.ds(pl.multiple_of(b * BLK, BLK), BLK)
                out_ref[:, at] = final(at)

            if nodes % BLK:
                low = nodes // BLK * BLK
                out_ref[:, low:nodes] = final(slice(low, low + BLK))[:, 0 : nodes - low]


def shards(
    wavefunctions,
    kinetic,
    cell_scale,
    potential,
    cell_nodes,
    face_space,
    face_slab,
    projectors,
    cell_atom,
    coupling,
):
    width, nodes = wavefunctions.shape
    cells, order = cell_nodes.shape
    atoms, nproj = coupling.shape[0], coupling.shape[1]
    n_space, n_slab = lax.axis_size("space"), lax.axis_size("slab")
    fs, fl = face_space.shape[1], face_slab.shape[1]
    pstride = up(nproj, 16)
    while cells * pstride % 128:
        pstride += 16
    dims = dict(
        n_space=n_space, n_slab=n_slab, width=width, nodes=nodes, cells=cells, order=order,
        atoms=atoms, nproj=nproj, pstride=pstride, fs=fs, fl=fl,
    )
    op, npad = up(order, BLK), up(nodes, BLK)
    fsp, flp = up(fs, 128), up(fl, 128)
    jp = cells * op
    fp = up(2 * fsp + 2 * flp, BLK)
    lp = cells * pstride
    others = max(n_slab - 1, 1)
    vmem = pl.BlockSpec(memory_space=pltpu.VMEM)
    smem = pl.BlockSpec(memory_space=pltpu.SMEM)
    dma = pltpu.SemaphoreType.DMA
    return pl.pallas_call(
        functools.partial(kernel, dims),
        out_shape=jax.ShapeDtypeStruct((width, nodes), f32),
        in_specs=[vmem, vmem, smem] + [vmem] * 5 + [smem, vmem],
        out_specs=vmem,
        scratch_shapes=[
            pltpu.VMEM((npad, jp), bf16),
            pltpu.VMEM((npad, fp), bf16),
            pltpu.VMEM((atoms * pstride + 8, lp), f32),
            pltpu.VMEM((8, jp + fp), jnp.int32),
            pltpu.VMEM((op, op), bf16),
            pltpu.VMEM((lp, jp), bf16),
            pltpu.VMEM((up(cells, 8), op), f32),
            pltpu.VMEM((2 * fsp, 2 * flp), bf16),
            pltpu.VMEM((others, atoms * pstride + 8, lp), f32),
            pltpu.VMEM((n_slab, lp, lp), f32),
            pltpu.VMEM((width, npad), bf16),
            pltpu.VMEM((cells * width, op), bf16),
            pltpu.VMEM((2 * width, jp), bf16),
            pltpu.VMEM((width, max(jp, npad)), f32),
            pltpu.VMEM((width, npad), bf16),
            pltpu.VMEM((width, npad), f32),
            pltpu.VMEM((2, width, fp), bf16),
            pltpu.VMEM((2, 2, width, fsp), bf16),
            pltpu.VMEM((2, 2, width, flp), bf16),
            pltpu.VMEM((width, fp), bf16),
            pltpu.VMEM((2, n_slab, width, lp), f32),
            dma((others,)),
            dma((others,)),
            dma((2, others)),
            dma((2, others)),
            dma((2, 4)),
            dma((2, 4)),
        ],
        compiler_params=pltpu.CompilerParams(
            collective_id=0, has_side_effects=True, vmem_limit_bytes=60 * 1024 * 1024
        ),
    )(
        wavefunctions, kinetic, cell_scale, potential, cell_nodes, face_space, face_slab,
        projectors.transpose(1, 0, 2), cell_atom, coupling.transpose(1, 0, 2),
    )


def solution(mesh):
    placed = (
        P(None, ("space", "slab")),
        P(),
        P(("space", "slab")),
        P(("space", "slab"), None),
        P(("space", "slab"), None),
        P(("space", "slab"), None),
        P(("space", "slab"), None),
        P(("space", "slab"), None, None),
        P(("space", "slab")),
        P(("space", "slab"), None, None),
    )
    return jax.shard_map(
        shards, mesh=mesh, in_specs=placed, out_specs=P(None, ("space", "slab")), check_vma=False
    )
```

```python
import functools

import jax
import jax.numpy as jnp
from jax import lax
from jax.experimental import pallas as pl
from jax.experimental.pallas import tpu as pltpu
from jax.sharding import PartitionSpec as P

filter_centre = 8.0
filter_half = 8.0
BLK = 256
MESH = pl.DeviceIdType.MESH
NT = (((1,), (1,)), ((), ()))
f32 = jnp.float32
bf16 = jnp.bfloat16


def up(value, unit):
    return -(-value // unit) * unit


def kernel(
    dims,
    y_ref,
    kin_ref,
    scale_ref,
    pot_ref,
    cn_ref,
    fs_ref,
    fl_ref,
    pr_ref,
    atom_ref,
    coupling_ref,
    out_ref,
    hot,
    hotf,
    hote,
    pack,
    idx,
    kin,
    pp,
    pot,
    cross,
    fcol,
    packs,
    coup,
    yb,
    vals,
    tot,
    asm,
    zhl,
    asm2,
    outg,
    in_space,
    in_slab,
    inc,
    marg,
    pack_send,
    pack_recv,
    marg_send,
    marg_recv,
    face_send,
    face_recv,
):
    n_space, n_slab = dims["n_space"], dims["n_slab"]
    width, nodes, cells, order = dims["width"], dims["nodes"], dims["cells"], dims["order"]
    atoms, nproj, pstride = dims["atoms"], dims["nproj"], dims["pstride"]
    fs, fl = dims["fs"], dims["fl"]
    op, npad = up(order, BLK), up(nodes, BLK)
    fsp, flp = up(fs, 128), up(fl, 128)
    jp = cells * op
    fp = up(2 * fsp + 2 * flp, BLK)
    lp = cells * pstride
    o_sl = 2 * fsp

    s = lax.axis_index("space")
    l = lax.axis_index("slab")
    above, below = lax.rem(s + 1, n_space), lax.rem(s + n_space - 1, n_space)
    right, left = lax.rem(l + 1, n_slab), lax.rem(l + n_slab - 1, n_slab)

    lane_cell = lax.broadcasted_iota(jnp.int32, (8, lp), 1) // pstride
    atom_row = jnp.zeros((8, lp), f32)
    for c in range(cells):
        atom_row = jnp.where(lane_cell == c, atom_ref[c].astype(f32), atom_row)
    pack[...] = jnp.zeros(pack.shape, f32)
    for i in range(atoms):
        part = slice(i * pstride, (i + 1) * pstride)
        pack[i * pstride : i * pstride + nproj, 0:nproj] = coupling_ref[:, i, :]
        once = pack[part, :]
        many = once
        for c in range(1, cells):
            many = many + pltpu.roll(once, c * pstride, 1)
        pack[part, :] = many
    pack[atoms * pstride :, :] = atom_row

    barrier = pltpu.get_barrier_semaphore()
    for d in range(1, n_slab):
        pl.semaphore_signal(
            barrier, inc=1, device_id={"slab": lax.rem(l + d, n_slab)}, device_id_type=MESH
        )
    for t in (above, below):
        pl.semaphore_signal(barrier, inc=1, device_id={"space": t}, device_id_type=MESH)
    idx[...] = jnp.full(idx.shape, -1, jnp.int32)
    for c in range(cells):
        idx[0:1, c * op : c * op + order] = cn_ref[c : c + 1, :]
    for k in range(2):
        idx[0:1, jp + k * fsp : jp + k * fsp + fs] = fs_ref[k : k + 1, :]
        off = jp + o_sl + k * flp
        idx[0:1, off : off + fl] = fl_ref[k : k + 1, :]

    kin[...] = jnp.zeros(kin.shape, bf16)
    kin[0:order, 0:order] = kin_ref[...]
    pp[...] = jnp.zeros(pp.shape, bf16)
    pot[...] = jnp.zeros(pot.shape, f32)
    pot[0:cells, 0:order] = pot_ref[...]
    yb[...] = jnp.zeros(yb.shape, bf16)
    yb[:, 0:nodes] = y_ref[...]
    for c in range(cells):
        pp[c * pstride : c * pstride + nproj, c * op : c * op + order] = pr_ref[:, c, :]

    rows = lax.broadcasted_iota(jnp.int32, (BLK, BLK), 0).astype(f32).astype(bf16)

    def one_hot(index_row, b):
        shifted = (index_row - b * BLK).astype(f32).astype(bf16)
        hit = rows == jnp.broadcast_to(shifted, (BLK, BLK))
        return jnp.where(hit, jnp.ones((), bf16), jnp.zeros((), bf16))

    slab_row = idx[0:1, jp + o_sl : jp + o_sl + 2 * flp].astype(f32)
    slab_row = jnp.where(slab_row < 0, -2.0, slab_row)
    for k in range(fp // 128):
        row = idx[0:1, jp + k * 128 : jp + (k + 1) * 128].astype(f32)
        col = jnp.broadcast_to(row, (128, 128)).T
        col = jnp.where(col < 0, -3.0, col)
        fcol[k * 128 : (k + 1) * 128, :] = col
        if k < 2 * fsp // 128:
            cross[k * 128 : (k + 1) * 128, :] = jnp.where(col[:, 0:1] == slab_row, 1.0, 0.0).astype(bf16)

    per_cell = op // BLK

    def build_gather(j):
        at = pl.ds(pl.multiple_of(j * BLK, BLK), BLK)
        index_row = idx[0:1, at]
        got = jnp.zeros((width, BLK), f32)
        for b in range(npad // BLK):
            part = slice(b * BLK, (b + 1) * BLK)
            block = one_hot(index_row, b)
            hot[part, at] = block
            got += jnp.dot(yb[:, part], block, preferred_element_type=f32)
        row = pl.ds(pl.multiple_of(j // per_cell * width, width), width)
        to = pl.ds(pl.multiple_of(j % per_cell * BLK, BLK), BLK)
        vals[row, to] = got.astype(bf16)
        for h in range(BLK // 128):
            lane = pl.ds(pl.multiple_of(j * BLK + h * 128, 128), 128)
            cell_row = jnp.broadcast_to(idx[0:1, lane].astype(f32), (128, 128))
            for k in range(fp // 128):
                part = slice(k * 128, (k + 1) * 128)
                hote[part, lane] = jnp.where(fcol[part, :] == cell_row, 1.0, 0.0).astype(bf16)

    half = cells * per_cell // 2
    pl.loop(0, half)(build_gather)
    pl.semaphore_wait(barrier, n_slab + 1)
    pack_copies = []
    for d in range(1, n_slab):
        copy = pltpu.make_async_remote_copy(
            src_ref=pack,
            dst_ref=packs.at[d - 1],
            send_sem=pack_send.at[d - 1],
            recv_sem=pack_recv.at[d - 1],
            device_id={"slab": lax.rem(l + d, n_slab)},
            device_id_type=MESH,
        )
        copy.start()
        pack_copies.append(copy)

    pl.loop(half, cells * per_cell)(build_gather)

    for copy in pack_copies:
        copy.wait()
    own_row = pack[atoms * pstride : atoms * pstride + 1, :]
    own_col = jnp.broadcast_to(own_row, (lp, lp)).T
    chosen = jnp.zeros((lp, lp), f32)
    for d in range(n_slab):
        source = lax.rem(l + n_slab - d, n_slab)
        for i in range(atoms):
            part = slice(i * pstride, (i + 1) * pstride)
            block = pack[part, :] if d == 0 else packs[d - 1, part, :]
            tiled = jnp.concatenate([block] * cells, axis=0)
            chosen += jnp.where(own_col == (source * atoms + i).astype(f32), tiled, 0.0)
    for d in range(n_slab):
        last = slice(atoms * pstride, atoms * pstride + 1)
        row = pack[last, :] if d == 0 else packs[d - 1, last, :]
        coup[d] = jnp.where(own_col == row, chosen, 0.0)

    lanes = lax.broadcasted_iota(jnp.int32, (1, fp), 1)
    has_below, has_above = s > 0, s < n_space - 1
    has_left, has_right = l > 0, l < n_slab - 1
    keep = (
        ((lanes < fsp) & has_below)
        | ((lanes >= fsp) & (lanes < o_sl) & has_above)
        | ((lanes >= o_sl) & (lanes < o_sl + flp) & has_left)
        | ((lanes >= o_sl + flp) & (lanes < o_sl + 2 * flp) & has_right)
    ).astype(f32)

    inc[...] = jnp.zeros(inc.shape, bf16)

    def face_copy(step, which, src, landing, device):
        count = landing.shape[-1]
        return pltpu.make_async_remote_copy(
            src_ref=outg.at[step, :, src : src + count],
            dst_ref=landing.at[step, which % 2],
            send_sem=face_send.at[step, which],
            recv_sem=face_recv.at[step, which],
            device_id=device,
            device_id_type=MESH,
        )

    for step in range(2):
        margin = jnp.zeros((width, lp), f32)
        for c in range(cells):
            margin += lax.dot_general(
                vals[c * width : (c + 1) * width, :],
                pp[:, c * op : (c + 1) * op],
                NT,
                preferred_element_type=f32,
            )
        marg[step, 0] = margin
        marg_copies = []
        for d in range(1, n_slab):
            copy = pltpu.make_async_remote_copy(
                src_ref=marg.at[step, 0],
                dst_ref=marg.at[step, d],
                send_sem=marg_send.at[step, d - 1],
                recv_sem=marg_recv.at[step, d - 1],
                device_id={"slab": lax.rem(l + d, n_slab)},
                device_id_type=MESH,
            )
            copy.start()
            marg_copies.append(copy)

        asm_kin = jnp.dot(vals[...], kin[...], preferred_element_type=f32)
        for c in range(cells):
            v = vals[c * width : (c + 1) * width, :].astype(f32)
            asm[:, c * op : (c + 1) * op] = (
                scale_ref[c] * asm_kin[c * width : (c + 1) * width] + pot[c : c + 1, :] * v
            )
        coupled = lax.dot_general(
            margin, coup[0], NT, precision=lax.Precision.HIGHEST, preferred_element_type=f32
        )
        for d in range(1, n_slab):
            marg_copies[d - 1].wait()
            coupled += lax.dot_general(
                marg[step, d], coup[d], NT, precision=lax.Precision.HIGHEST, preferred_element_type=f32
            )
        coupled = coupled.astype(bf16)
        for c in range(cells):
            cols = slice(c * op, (c + 1) * op)
            total = asm[:, cols] + jnp.dot(coupled, pp[:, cols], preferred_element_type=f32)
            high = total.astype(bf16)
            tot[0:width, cols] = high
            tot[width:, cols] = (total - high.astype(f32)).astype(bf16)

        @pl.loop(0, fp // BLK)
        def _(b):
            to = pl.ds(pl.multiple_of(b * BLK, BLK), BLK)
            both = lax.dot_general(tot[:, 0:jp], hote[to, :], NT, preferred_element_type=f32)
            outg[step, :, to] = (both[0:width] + both[width:]).astype(bf16)

        space_copies = [
            face_copy(step, 0, fsp, in_space, {"space": above}),
            face_copy(step, 1, 0, in_space, {"space": below}),
        ]
        for copy in space_copies:
            copy.start()

        def scatter(b, step=step):
            at = pl.ds(pl.multiple_of(b * BLK, BLK), BLK)
            if step == 0:
                for j in range(fp // BLK):
                    hotf[at, j * BLK : (j + 1) * BLK] = one_hot(
                        idx[0:1, jp + j * BLK : jp + (j + 1) * BLK], b
                    )
            both = lax.dot_general(tot[:, 0:jp], hot[at, :], NT, preferred_element_type=f32)
            summed = both[0:width] + both[width:]
            if step == 0:
                start = yb[:, at].astype(f32)
                partial = (summed - filter_centre * start) / filter_half
                high = partial.astype(bf16)
                zhl[0:width, at] = high
                zhl[width:, at] = (partial - high.astype(f32)).astype(bf16)
                asm2[:, at] = -2.0 * filter_centre * partial / filter_half - start
            else:
                asm2[:, at] += 2.0 * summed / filter_half

        blocks = npad // BLK
        first = blocks if step == 0 else blocks // 2
        pl.loop(0, first)(scatter)

        for k, copy in enumerate(space_copies):
            copy.wait()
            part = slice(k * fsp, (k + 1) * fsp)
            inc[step, :, part] = (in_space[step, k].astype(f32) * keep[:, part]).astype(bf16)
        extra = jnp.dot(inc[step, :, 0:o_sl], cross[...], preferred_element_type=f32)
        part = slice(o_sl, o_sl + 2 * flp)
        outg[step, :, part] = (outg[step, :, part].astype(f32) + extra).astype(bf16)
        slab_copies = [
            face_copy(step, 2, o_sl + flp, in_slab, {"slab": right}),
            face_copy(step, 3, o_sl, in_slab, {"slab": left}),
        ]
        for copy in slab_copies:
            copy.start()

        if step == 0:
            @pl.loop(0, cells * per_cell)
            def _(j):
                at = pl.ds(pl.multiple_of(j * BLK, BLK), BLK)
                both = jnp.dot(zhl[...], hot[:, at], preferred_element_type=f32)
                asm[:, at] = both[0:width] + both[width:]
        else:
            pl.loop(first, blocks)(scatter)

        for k, copy in enumerate(slab_copies):
            copy.wait()
            part = slice(o_sl + k * flp, o_sl + (k + 1) * flp)
            inc[step, :, part] = (in_slab[step, k].astype(f32) * keep[:, part]).astype(bf16)

        if step == 0:
            @pl.loop(0, cells * per_cell)
            def _(j):
                at = pl.ds(pl.multiple_of(j * BLK, BLK), BLK)
                added = jnp.dot(inc[0], hote[:, at], preferred_element_type=f32)
                row = pl.ds(pl.multiple_of(j // per_cell * width, width), width)
                to = pl.ds(pl.multiple_of(j % per_cell * BLK, BLK), BLK)
                vals[row, to] = (asm[:, at] + added / filter_half).astype(bf16)

    change = (
        2.0 / filter_half * inc[1].astype(f32)
        - 2.0 * filter_centre / filter_half / filter_half * inc[0].astype(f32)
    )
    high = change.astype(bf16)
    tot[0:width, 0:fp] = high
    tot[width:, 0:fp] = (change - high.astype(f32)).astype(bf16)

    def final(at):
        both = lax.dot_general(tot[:, 0:fp], hotf[at, :], NT, preferred_element_type=f32)
        return asm2[:, at] + both[0:width] + both[width:]

    @pl.loop(0, nodes // BLK)
    def _(b):
        at = pl.ds(pl.multiple_of(b * BLK, BLK), BLK)
        out_ref[:, at] = final(at)

    if nodes % BLK:
        low = nodes // BLK * BLK
        out_ref[:, low:nodes] = final(slice(low, low + BLK))[:, 0 : nodes - low]


def shards(
    wavefunctions,
    kinetic,
    cell_scale,
    potential,
    cell_nodes,
    face_space,
    face_slab,
    projectors,
    cell_atom,
    coupling,
):
    width, nodes = wavefunctions.shape
    cells, order = cell_nodes.shape
    atoms, nproj = coupling.shape[0], coupling.shape[1]
    n_space, n_slab = lax.axis_size("space"), lax.axis_size("slab")
    fs, fl = face_space.shape[1], face_slab.shape[1]
    pstride = up(nproj, 16)
    while cells * pstride % 128:
        pstride += 16
    dims = dict(
        n_space=n_space, n_slab=n_slab, width=width, nodes=nodes, cells=cells, order=order,
        atoms=atoms, nproj=nproj, pstride=pstride, fs=fs, fl=fl,
    )
    op, npad = up(order, BLK), up(nodes, BLK)
    fsp, flp = up(fs, 128), up(fl, 128)
    jp = cells * op
    fp = up(2 * fsp + 2 * flp, BLK)
    lp = cells * pstride
    others = max(n_slab - 1, 1)
    vmem = pl.BlockSpec(memory_space=pltpu.VMEM)
    smem = pl.BlockSpec(memory_space=pltpu.SMEM)
    dma = pltpu.SemaphoreType.DMA
    return pl.pallas_call(
        functools.partial(kernel, dims),
        out_shape=jax.ShapeDtypeStruct((width, nodes), f32),
        in_specs=[vmem, vmem, smem] + [vmem] * 5 + [smem, vmem],
        out_specs=vmem,
        scratch_shapes=[
            pltpu.VMEM((npad, jp), bf16),
            pltpu.VMEM((npad, fp), bf16),
            pltpu.VMEM((fp, jp), bf16),
            pltpu.VMEM((atoms * pstride + 8, lp), f32),
            pltpu.VMEM((8, jp + fp), jnp.int32),
            pltpu.VMEM((op, op), bf16),
            pltpu.VMEM((lp, jp), bf16),
            pltpu.VMEM((up(cells, 8), op), f32),
            pltpu.VMEM((2 * fsp, 2 * flp), bf16),
            pltpu.VMEM((fp, 128), f32),
            pltpu.VMEM((others, atoms * pstride + 8, lp), f32),
            pltpu.VMEM((n_slab, lp, lp), f32),
            pltpu.VMEM((width, npad), bf16),
            pltpu.VMEM((cells * width, op), bf16),
            pltpu.VMEM((2 * width, max(jp, fp)), bf16),
            pltpu.VMEM((width, jp), f32),
            pltpu.VMEM((2 * width, npad), bf16),
            pltpu.VMEM((width, npad), f32),
            pltpu.VMEM((2, width, fp), bf16),
            pltpu.VMEM((2, 2, width, fsp), bf16),
            pltpu.VMEM((2, 2, width, flp), bf16),
            pltpu.VMEM((2, width, fp), bf16),
            pltpu.VMEM((2, n_slab, width, lp), f32),
            dma((others,)),
            dma((others,)),
            dma((2, others)),
            dma((2, others)),
            dma((2, 4)),
            dma((2, 4)),
        ],
        compiler_params=pltpu.CompilerParams(
            collective_id=0, has_side_effects=True, vmem_limit_bytes=60 * 1024 * 1024
        ),
    )(
        wavefunctions, kinetic, cell_scale, potential, cell_nodes, face_space, face_slab,
        projectors.transpose(1, 0, 2), cell_atom, coupling.transpose(1, 0, 2),
    )


def solution(mesh):
    placed = (
        P(None, ("space", "slab")),
        P(),
        P(("space", "slab")),
        P(("space", "slab"), None),
        P(("space", "slab"), None),
        P(("space", "slab"), None),
        P(("space", "slab"), None),
        P(("space", "slab"), None, None),
        P(("space", "slab")),
        P(("space", "slab"), None, None),
    )
    return jax.shard_map(
        shards, mesh=mesh, in_specs=placed, out_specs=P(None, ("space", "slab")), check_vma=False
    )
```

```python
import functools

import jax
import jax.numpy as jnp
from jax import lax
from jax.experimental import pallas as pl
from jax.experimental.pallas import tpu as pltpu
from jax.sharding import PartitionSpec as P

filter_centre = 8.0
filter_half = 8.0
BLK = 256
MESH = pl.DeviceIdType.MESH
NT = (((1,), (1,)), ((), ()))
f32 = jnp.float32
bf16 = jnp.bfloat16


def up(value, unit):
    return -(-value // unit) * unit


def kernel(
    dims,
    y_ref,
    kin_ref,
    scale_ref,
    pot_ref,
    cn_ref,
    fs_ref,
    fl_ref,
    pr_ref,
    atom_ref,
    coupling_ref,
    out_ref,
    hot,
    hotf,
    hote,
    dup,
    pack,
    idx,
    kin,
    pp,
    pot,
    cross,
    fcol,
    packs,
    coup,
    yb,
    vals,
    tot,
    asm,
    uhl,
    first_total,
    asm2,
    outg,
    in_space,
    in_slab,
    inc,
    marg,
    pack_send,
    pack_recv,
    marg_send,
    marg_recv,
    face_send,
    face_recv,
):
    n_space, n_slab = dims["n_space"], dims["n_slab"]
    width, nodes, cells, order = dims["width"], dims["nodes"], dims["cells"], dims["order"]
    atoms, nproj, pstride = dims["atoms"], dims["nproj"], dims["pstride"]
    fs, fl = dims["fs"], dims["fl"]
    op, npad = up(order, BLK), up(nodes, BLK)
    fsp, flp = up(fs, 128), up(fl, 128)
    jp = cells * op
    fp = up(2 * fsp + 2 * flp, BLK)
    lp = cells * pstride
    o_sl = 2 * fsp

    s = lax.axis_index("space")
    l = lax.axis_index("slab")
    above, below = lax.rem(s + 1, n_space), lax.rem(s + n_space - 1, n_space)
    right, left = lax.rem(l + 1, n_slab), lax.rem(l + n_slab - 1, n_slab)

    lane_cell = lax.broadcasted_iota(jnp.int32, (8, lp), 1) // pstride
    atom_row = jnp.zeros((8, lp), f32)
    for c in range(cells):
        atom_row = jnp.where(lane_cell == c, atom_ref[c].astype(f32), atom_row)
    pack[...] = jnp.zeros(pack.shape, f32)
    for i in range(atoms):
        part = slice(i * pstride, (i + 1) * pstride)
        pack[i * pstride : i * pstride + nproj, 0:nproj] = coupling_ref[:, i, :]
        once = pack[part, :]
        many = once
        for c in range(1, cells):
            many = many + pltpu.roll(once, c * pstride, 1)
        pack[part, :] = many
    pack[atoms * pstride :, :] = atom_row

    barrier = pltpu.get_barrier_semaphore()
    for d in range(1, n_slab):
        pl.semaphore_signal(
            barrier, inc=1, device_id={"slab": lax.rem(l + d, n_slab)}, device_id_type=MESH
        )
    for t in (above, below):
        pl.semaphore_signal(barrier, inc=1, device_id={"space": t}, device_id_type=MESH)
    idx[...] = jnp.full(idx.shape, -1, jnp.int32)
    for c in range(cells):
        idx[0:1, c * op : c * op + order] = cn_ref[c : c + 1, :]
    for k in range(2):
        idx[0:1, jp + k * fsp : jp + k * fsp + fs] = fs_ref[k : k + 1, :]
        off = jp + o_sl + k * flp
        idx[0:1, off : off + fl] = fl_ref[k : k + 1, :]

    kin[...] = jnp.zeros(kin.shape, bf16)
    kin[0:order, 0:order] = kin_ref[...]
    pp[...] = jnp.zeros(pp.shape, bf16)
    pot[...] = jnp.zeros(pot.shape, f32)
    pot[0:cells, 0:order] = pot_ref[...]
    yb[...] = jnp.zeros(yb.shape, bf16)
    yb[:, 0:nodes] = y_ref[...]
    for c in range(cells):
        pp[c * pstride : c * pstride + nproj, c * op : c * op + order] = pr_ref[:, c, :]

    rows = lax.broadcasted_iota(jnp.int32, (BLK, BLK), 0).astype(f32).astype(bf16)

    def one_hot(index_row, b):
        shifted = (index_row - b * BLK).astype(f32).astype(bf16)
        hit = rows == jnp.broadcast_to(shifted, (BLK, BLK))
        return jnp.where(hit, jnp.ones((), bf16), jnp.zeros((), bf16))

    slab_row = idx[0:1, jp + o_sl : jp + o_sl + 2 * flp].astype(f32)
    slab_row = jnp.where(slab_row < 0, -2.0, slab_row)
    for k in range(fp // 128):
        row = idx[0:1, jp + k * 128 : jp + (k + 1) * 128].astype(f32)
        col = jnp.broadcast_to(row, (128, 128)).T
        col = jnp.where(col < 0, -3.0, col)
        fcol[k * 128 : (k + 1) * 128, :] = col
        if k < 2 * fsp // 128:
            cross[k * 128 : (k + 1) * 128, :] = jnp.where(col[:, 0:1] == slab_row, 1.0, 0.0).astype(bf16)

    per_cell = op // BLK

    def build_gather(j):
        at = pl.ds(pl.multiple_of(j * BLK, BLK), BLK)
        index_row = idx[0:1, at]
        got = jnp.zeros((width, BLK), f32)
        for b in range(npad // BLK):
            part = slice(b * BLK, (b + 1) * BLK)
            block = one_hot(index_row, b)
            hot[part, at] = block
            got += jnp.dot(yb[:, part], block, preferred_element_type=f32)
        row = pl.ds(pl.multiple_of(j // per_cell * width, width), width)
        to = pl.ds(pl.multiple_of(j % per_cell * BLK, BLK), BLK)
        vals[row, to] = got.astype(bf16)
        for h in range(BLK // 128):
            lane = pl.ds(pl.multiple_of(j * BLK + h * 128, 128), 128)
            cell_row = jnp.broadcast_to(idx[0:1, lane].astype(f32), (128, 128))
            for k in range(fp // 128):
                part = slice(k * 128, (k + 1) * 128)
                hote[part, lane] = jnp.where(fcol[part, :] == cell_row, 1.0, 0.0).astype(bf16)

    n_pairs = cells * (cells - 1) // 2
    hop = op // 2

    def build_dup(u):
        q, hf = u // 2, u % 2
        one = q % cells
        two = (one + 1 + q // cells) % cells
        for k in range(hop // 128):
            lane = pl.ds(pl.multiple_of(one * op + hf * hop + k * 128, 128), 128)
            col = jnp.broadcast_to(idx[0:1, lane].astype(f32), (128, 128)).T
            col = jnp.where(col < 0, -2.0, col)
            to = pl.ds(pl.multiple_of(q * op + hf * hop + k * 128, 128), 128)
            for h in range(op // 128):
                lane = pl.ds(pl.multiple_of(two * op + h * 128, 128), 128)
                row = jnp.broadcast_to(idx[0:1, lane].astype(f32), (128, 128))
                dup[to, h * 128 : (h + 1) * 128] = jnp.where(col == row, 1.0, 0.0).astype(bf16)

    together = 2 * n_pairs == cells * per_cell

    def build_all(j):
        build_gather(j)
        if together:
            build_dup(j)

    if not together:
        pl.loop(0, 2 * n_pairs)(build_dup)
    half = cells * per_cell // 2
    pl.loop(0, half)(build_all)
    pl.semaphore_wait(barrier, n_slab + 1)
    pack_copies = []
    for d in range(1, n_slab):
        copy = pltpu.make_async_remote_copy(
            src_ref=pack,
            dst_ref=packs.at[d - 1],
            send_sem=pack_send.at[d - 1],
            recv_sem=pack_recv.at[d - 1],
            device_id={"slab": lax.rem(l + d, n_slab)},
            device_id_type=MESH,
        )
        copy.start()
        pack_copies.append(copy)

    pl.loop(half, cells * per_cell)(build_all)

    for copy in pack_copies:
        copy.wait()
    own_row = pack[atoms * pstride : atoms * pstride + 1, :]
    own_col = jnp.broadcast_to(own_row, (lp, lp)).T
    chosen = jnp.zeros((lp, lp), f32)
    for d in range(n_slab):
        source = lax.rem(l + n_slab - d, n_slab)
        for i in range(atoms):
            part = slice(i * pstride, (i + 1) * pstride)
            block = pack[part, :] if d == 0 else packs[d - 1, part, :]
            tiled = jnp.concatenate([block] * cells, axis=0)
            chosen += jnp.where(own_col == (source * atoms + i).astype(f32), tiled, 0.0)
    for d in range(n_slab):
        last = slice(atoms * pstride, atoms * pstride + 1)
        row = pack[last, :] if d == 0 else packs[d - 1, last, :]
        coup[d] = jnp.where(own_col == row, chosen, 0.0)

    lanes = lax.broadcasted_iota(jnp.int32, (1, fp), 1)
    has_below, has_above = s > 0, s < n_space - 1
    has_left, has_right = l > 0, l < n_slab - 1
    keep = (
        ((lanes < fsp) & has_below)
        | ((lanes >= fsp) & (lanes < o_sl) & has_above)
        | ((lanes >= o_sl) & (lanes < o_sl + flp) & has_left)
        | ((lanes >= o_sl + flp) & (lanes < o_sl + 2 * flp) & has_right)
    ).astype(f32)

    inc[...] = jnp.zeros(inc.shape, bf16)

    def face_copy(step, which, src, landing, device):
        count = landing.shape[-1]
        return pltpu.make_async_remote_copy(
            src_ref=outg.at[step, :, src : src + count],
            dst_ref=landing.at[step, which % 2],
            send_sem=face_send.at[step, which],
            recv_sem=face_recv.at[step, which],
            device_id=device,
            device_id_type=MESH,
        )

    for step in range(2):
        margin = jnp.zeros((width, lp), f32)
        for c in range(cells):
            margin += lax.dot_general(
                vals[c * width : (c + 1) * width, :],
                pp[:, c * op : (c + 1) * op],
                NT,
                preferred_element_type=f32,
            )
        marg[step, 0] = margin
        marg_copies = []
        for d in range(1, n_slab):
            copy = pltpu.make_async_remote_copy(
                src_ref=marg.at[step, 0],
                dst_ref=marg.at[step, d],
                send_sem=marg_send.at[step, d - 1],
                recv_sem=marg_recv.at[step, d - 1],
                device_id={"slab": lax.rem(l + d, n_slab)},
                device_id_type=MESH,
            )
            copy.start()
            marg_copies.append(copy)

        asm_kin = jnp.dot(vals[...], kin[...], preferred_element_type=f32)
        for c in range(cells):
            v = vals[c * width : (c + 1) * width, :].astype(f32)
            asm[:, c * op : (c + 1) * op] = (
                scale_ref[c] * asm_kin[c * width : (c + 1) * width] + pot[c : c + 1, :] * v
            )
        coupled = lax.dot_general(
            margin, coup[0], NT, precision=lax.Precision.HIGHEST, preferred_element_type=f32
        )
        for d in range(1, n_slab):
            marg_copies[d - 1].wait()
            coupled += lax.dot_general(
                marg[step, d], coup[d], NT, precision=lax.Precision.HIGHEST, preferred_element_type=f32
            )
        coupled = coupled.astype(bf16)
        for c in range(cells):
            cols = slice(c * op, (c + 1) * op)
            total = asm[:, cols] + jnp.dot(coupled, pp[:, cols], preferred_element_type=f32)
            high = total.astype(bf16)
            tot[0:width, cols] = high
            tot[width:, cols] = (total - high.astype(f32)).astype(bf16)
            if step == 0:
                first_total[:, cols] = total
            else:
                step_change = 2.0 / filter_half * total - (
                    2.0 * filter_centre / filter_half / filter_half * first_total[:, cols]
                )
                high = step_change.astype(bf16)
                uhl[0:width, cols] = high
                uhl[width:, cols] = (step_change - high.astype(f32)).astype(bf16)

        @pl.loop(0, fp // BLK)
        def _(b):
            to = pl.ds(pl.multiple_of(b * BLK, BLK), BLK)
            both = lax.dot_general(tot[:, 0:jp], hote[to, :], NT, preferred_element_type=f32)
            outg[step, :, to] = (both[0:width] + both[width:]).astype(bf16)

        space_copies = [
            face_copy(step, 0, fsp, in_space, {"space": above}),
            face_copy(step, 1, 0, in_space, {"space": below}),
        ]
        for copy in space_copies:
            copy.start()

        def scatter(b):
            at = pl.ds(pl.multiple_of(b * BLK, BLK), BLK)
            for j in range(fp // BLK):
                hotf[at, j * BLK : (j + 1) * BLK] = one_hot(
                    idx[0:1, jp + j * BLK : jp + (j + 1) * BLK], b
                )
            both = lax.dot_general(uhl[...], hot[at, :], NT, preferred_element_type=f32)
            start = yb[:, at].astype(f32)
            kept = 2.0 * filter_centre * filter_centre / filter_half / filter_half - 1.0
            asm2[:, at] = both[0:width] + both[width:] + kept * start

        def share(c):
            @pl.loop(0, per_cell)
            def _(n):
                to = pl.ds(pl.multiple_of(n * BLK, BLK), BLK)
                both = jnp.zeros((2 * width, BLK), f32)
                for q in range(n_pairs):
                    one = q % cells
                    two = (one + 1 + q // cells) % cells
                    if two == c:
                        both += jnp.dot(
                            tot[:, one * op : (one + 1) * op],
                            dup[q * op : (q + 1) * op, to],
                            preferred_element_type=f32,
                        )
                    elif one == c:
                        rows = pl.ds(pl.multiple_of(q * op + n * BLK, BLK), BLK)
                        both += lax.dot_general(
                            tot[:, two * op : (two + 1) * op],
                            dup[rows, :],
                            NT,
                            preferred_element_type=f32,
                        )
                at = pl.ds(pl.multiple_of(c * op + n * BLK, BLK), BLK)
                value = vals[c * width : (c + 1) * width, to].astype(f32)
                summed = first_total[:, at] + both[0:width] + both[width:]
                asm[:, at] = (summed - filter_centre * value) / filter_half

        blocks = npad // BLK
        if step == 0:
            for c in range(cells // 2):
                share(c)
        else:
            pl.loop(0, blocks // 2)(scatter)

        for k, copy in enumerate(space_copies):
            copy.wait()
            part = slice(k * fsp, (k + 1) * fsp)
            inc[step, :, part] = (in_space[step, k].astype(f32) * keep[:, part]).astype(bf16)
        extra = jnp.dot(inc[step, :, 0:o_sl], cross[...], preferred_element_type=f32)
        part = slice(o_sl, o_sl + 2 * flp)
        outg[step, :, part] = (outg[step, :, part].astype(f32) + extra).astype(bf16)
        slab_copies = [
            face_copy(step, 2, o_sl + flp, in_slab, {"slab": right}),
            face_copy(step, 3, o_sl, in_slab, {"slab": left}),
        ]
        for copy in slab_copies:
            copy.start()

        if step == 0:
            for c in range(cells // 2, cells):
                share(c)
        else:
            pl.loop(blocks // 2, blocks)(scatter)

        for k, copy in enumerate(slab_copies):
            copy.wait()
            part = slice(o_sl + k * flp, o_sl + (k + 1) * flp)
            inc[step, :, part] = (in_slab[step, k].astype(f32) * keep[:, part]).astype(bf16)

        if step == 0:
            @pl.loop(0, cells * per_cell)
            def _(j):
                at = pl.ds(pl.multiple_of(j * BLK, BLK), BLK)
                added = jnp.dot(inc[0], hote[:, at], preferred_element_type=f32)
                row = pl.ds(pl.multiple_of(j // per_cell * width, width), width)
                to = pl.ds(pl.multiple_of(j % per_cell * BLK, BLK), BLK)
                vals[row, to] = (asm[:, at] + added / filter_half).astype(bf16)

    change = (
        2.0 / filter_half * inc[1].astype(f32)
        - 2.0 * filter_centre / filter_half / filter_half * inc[0].astype(f32)
    )
    high = change.astype(bf16)
    tot[0:width, 0:fp] = high
    tot[width:, 0:fp] = (change - high.astype(f32)).astype(bf16)

    def final(at):
        both = lax.dot_general(tot[:, 0:fp], hotf[at, :], NT, preferred_element_type=f32)
        return asm2[:, at] + both[0:width] + both[width:]

    @pl.loop(0, nodes // BLK)
    def _(b):
        at = pl.ds(pl.multiple_of(b * BLK, BLK), BLK)
        out_ref[:, at] = final(at)

    if nodes % BLK:
        low = nodes // BLK * BLK
        out_ref[:, low:nodes] = final(slice(low, low + BLK))[:, 0 : nodes - low]


def shards(
    wavefunctions,
    kinetic,
    cell_scale,
    potential,
    cell_nodes,
    face_space,
    face_slab,
    projectors,
    cell_atom,
    coupling,
):
    width, nodes = wavefunctions.shape
    cells, order = cell_nodes.shape
    atoms, nproj = coupling.shape[0], coupling.shape[1]
    n_space, n_slab = lax.axis_size("space"), lax.axis_size("slab")
    fs, fl = face_space.shape[1], face_slab.shape[1]
    pstride = up(nproj, 16)
    while cells * pstride % 128:
        pstride += 16
    dims = dict(
        n_space=n_space, n_slab=n_slab, width=width, nodes=nodes, cells=cells, order=order,
        atoms=atoms, nproj=nproj, pstride=pstride, fs=fs, fl=fl,
    )
    op, npad = up(order, BLK), up(nodes, BLK)
    fsp, flp = up(fs, 128), up(fl, 128)
    jp = cells * op
    fp = up(2 * fsp + 2 * flp, BLK)
    lp = cells * pstride
    others = max(n_slab - 1, 1)
    vmem = pl.BlockSpec(memory_space=pltpu.VMEM)
    smem = pl.BlockSpec(memory_space=pltpu.SMEM)
    dma = pltpu.SemaphoreType.DMA
    return pl.pallas_call(
        functools.partial(kernel, dims),
        out_shape=jax.ShapeDtypeStruct((width, nodes), f32),
        in_specs=[vmem, vmem, smem] + [vmem] * 5 + [smem, vmem],
        out_specs=vmem,
        scratch_shapes=[
            pltpu.VMEM((npad, jp), bf16),
            pltpu.VMEM((npad, fp), bf16),
            pltpu.VMEM((fp, jp), bf16),
            pltpu.VMEM((cells * (cells - 1) // 2 * op, op), bf16),
            pltpu.VMEM((atoms * pstride + 8, lp), f32),
            pltpu.VMEM((8, jp + fp), jnp.int32),
            pltpu.VMEM((op, op), bf16),
            pltpu.VMEM((lp, jp), bf16),
            pltpu.VMEM((up(cells, 8), op), f32),
            pltpu.VMEM((2 * fsp, 2 * flp), bf16),
            pltpu.VMEM((fp, 128), f32),
            pltpu.VMEM((others, atoms * pstride + 8, lp), f32),
            pltpu.VMEM((n_slab, lp, lp), f32),
            pltpu.VMEM((width, npad), bf16),
            pltpu.VMEM((cells * width, op), bf16),
            pltpu.VMEM((2 * width, max(jp, fp)), bf16),
            pltpu.VMEM((width, jp), f32),
            pltpu.VMEM((2 * width, jp), bf16),
            pltpu.VMEM((width, jp), f32),
            pltpu.VMEM((width, npad), f32),
            pltpu.VMEM((2, width, fp), bf16),
            pltpu.VMEM((2, 2, width, fsp), bf16),
            pltpu.VMEM((2, 2, width, flp), bf16),
            pltpu.VMEM((2, width, fp), bf16),
            pltpu.VMEM((2, n_slab, width, lp), f32),
            dma((others,)),
            dma((others,)),
            dma((2, others)),
            dma((2, others)),
            dma((2, 4)),
            dma((2, 4)),
        ],
        compiler_params=pltpu.CompilerParams(
            collective_id=0, has_side_effects=True, vmem_limit_bytes=60 * 1024 * 1024
        ),
    )(
        wavefunctions, kinetic, cell_scale, potential, cell_nodes, face_space, face_slab,
        projectors.transpose(1, 0, 2), cell_atom, coupling.transpose(1, 0, 2),
    )


def solution(mesh):
    placed = (
        P(None, ("space", "slab")),
        P(),
        P(("space", "slab")),
        P(("space", "slab"), None),
        P(("space", "slab"), None),
        P(("space", "slab"), None),
        P(("space", "slab"), None),
        P(("space", "slab"), None, None),
        P(("space", "slab")),
        P(("space", "slab"), None, None),
    )
    return jax.shard_map(
        shards, mesh=mesh, in_specs=placed, out_specs=P(None, ("space", "slab")), check_vma=False
    )
```
